256 devices in a mesh: rows: 4 (over y), past: 64 (over x, z, core).
Axes of the slice: x: 4, y: 4, z: 8, core: 2. Of those that a mesh axis runs over, the one named last changes fastest.
Arguments:
- tile_left: float32 [4, 64, 1024, 128], P('rows', 'past'), may hold values from -0.0625 to 0.0625
- tile_right: float32 [4, 64, 1024, 128], P('rows', 'past'), may hold values from -0.1875 to 0.1875
- diag_left: float32 [64, 1024, 128], P('past', 'rows'), may hold values from -6 to 6
- diag_right: float32 [64, 1024, 128], P('past', 'rows'), may hold values from -0.1875 to 0.1875
- present: int32 [4, 64], P('rows', 'past'), may hold values 0 or 1
- old_left: float32 [4, 1024, 128], P('rows'), may hold values from -6 to 6
- old_right: float32 [4, 1024, 128], P('rows'), may hold values from -0.1875 to 0.1875
- start: float32 [4, 1024, 128], P('rows'), may hold values from -6 to 6
Outputs:
- left: float32 [4, 1024, 128], P('rows')
- right: float32 [4, 1024, 128], P('rows')
The draws below stay inside these ranges and needn't reach their ends.
Inputs may be any that keep to these rules, and one draw needn't show every extreme that they name: present is 1 exactly where the past tile of that tile row and panel is listed.
All inputs are finite; a program needn't handle non-finite values. No bound on the sum of `present` on one device may be relied on, other than what follows from the above.
Results may differ from the reference program's by a relative error of at most 0.00026.
Values sent between devices are 32-bit elements; how exact they have to be, the bound alone decides.
No kernel may reach another device: no remote copies, remote signals or barrier semaphores. Data moves between devices by JAX's collectives and lax.ppermute only.
A program may use at most 64 MiB of HBM per device.

```python
import math
import jax
import jax.numpy as jnp
from jax import lax

B = 1024
R = 128
ITERS = 3
TROWS = 4
PAST = 64


def set_ends(drawn, key, smallest, top_value):
    longest = drawn.shape.index(max(drawn.shape))
    spots = []
    for shift in (0, 1):
        where = [jax.random.randint(jax.random.fold_in(key, axis), (), 0, length) for axis, length in enumerate(drawn.shape)]
        where[longest] = (where[longest] + shift) % drawn.shape[longest]
        spots.append(tuple(where))
    return drawn.at[spots[0]].set(smallest).at[spots[1]].set(top_value)


def levels(own_key, extent, cuts, low, largest):
    loudness = 1.0
    for dim, blocks in cuts:
        heights = jax.random.uniform(jax.random.fold_in(jax.random.fold_in(own_key, 6), dim), (blocks,), jnp.float32, low / len(cuts), largest / len(cuts))
        loudness = loudness * jnp.repeat(jnp.exp(heights), extent[dim] // blocks).reshape((-1,) + (1,) * (len(extent) - 1 - dim))
    return loudness


def centred(own_key, dims, scale, most, split=(), kind=jnp.bfloat16):
    factor_of = levels(own_key, dims, split, -0.22, 0.18) if split else 1.0
    entries = jax.random.normal(own_key, dims, jnp.float32) * scale * factor_of
    return jnp.minimum(jnp.maximum(entries, -most), most).astype(kind)


def setup_inputs(seed: int = 0) -> dict:
    splits = jax.random.split(jax.random.key(seed), 9)
    return {
        "tile_left": centred(splits[0], (TROWS, PAST, B, R), (R * PAST) ** -0.5, 0.0625, ((0, 4), (1, 64)), jnp.float32),
        "tile_right": centred(splits[1], (TROWS, PAST, B, R), B ** -0.5, 0.1875, ((0, 4), (1, 64)), jnp.float32),
        "diag_left": centred(splits[2], (PAST, B, R), 1.0, 6.0, ((0, 64), (1, 4)), jnp.float32),
        "diag_right": centred(splits[3], (PAST, B, R), B ** -0.5, 0.1875, ((0, 64), (1, 4)), jnp.float32),
        "present": set_ends((jax.random.randint(splits[4], (TROWS, PAST), 0, 4) < 3).astype(jnp.int32), jax.random.fold_in(splits[4], 1), 0, 1),
        "old_left": centred(splits[5], (TROWS, B, R), 1.0, 6.0, ((0, 4),), jnp.float32),
        "old_right": centred(splits[6], (TROWS, B, R), (8 * R) ** -0.5, 0.1875, ((0, 4),), jnp.float32),
        "start": centred(splits[7], (TROWS, B, R), 1.0, 6.0, ((0, 4),), jnp.float32),
    }


HIGH = lax.Precision.HIGHEST

def orthonormal(block):
    gram = jnp.dot(block.T, block, precision=HIGH)
    lower = jnp.linalg.cholesky(gram)
    inverse = jax.scipy.linalg.solve_triangular(lower, jnp.eye(block.shape[1], dtype=jnp.float32), lower=True)
    return jnp.dot(block, inverse.T, precision=HIGH)

def reference(tile_left, tile_right, diag_left, diag_right, present, old_left, old_right, start):
    weights = present.astype(jnp.float32)

    def one_row(items):
        left_row, right_row, mask_row, old_l, old_r, begin = items
        coupling = jnp.einsum('pbr,pbs->prs', right_row, diag_right, precision=HIGH) * mask_row[:, None, None]

        def forward(block):
            inner = jnp.einsum('pbs,bt->pst', diag_left, block, precision=HIGH)
            middle = jnp.einsum('prs,pst->prt', coupling, inner, precision=HIGH)
            summed = jnp.einsum('pbr,prt->bt', left_row, middle, precision=HIGH)
            return jnp.dot(old_l, jnp.dot(old_r.T, block, precision=HIGH), precision=HIGH) - summed

        def backward(block):
            inner = jnp.einsum('pbr,bt->prt', left_row, block, precision=HIGH)
            middle = jnp.einsum('prs,prt->pst', coupling, inner, precision=HIGH)
            summed = jnp.einsum('pbs,pst->bt', diag_left, middle, precision=HIGH)
            return jnp.dot(old_r, jnp.dot(old_l.T, block, precision=HIGH), precision=HIGH) - summed
        basis = orthonormal(forward(begin))
        for sweep in range(ITERS):
            basis = orthonormal(forward(orthonormal(backward(basis))))
        return (basis * math.sqrt(B), backward(basis))
    return lax.map(one_row, (tile_left, tile_right, weights, old_left, old_right, start))
```

```python
import math

import jax
import jax.numpy as jnp
from jax import lax
from jax.experimental import pallas as pl
from jax.experimental.pallas import tpu as pltpu
from jax.sharding import PartitionSpec as P

B = 1024
R = 128
ITERS = 3
NB = 8

HIGH = lax.Precision.HIGHEST
NN = (((1,), (0,)), ((), ()))
NT = (((1,), (1,)), ((), ()))


def lane(block, k):
    return jnp.broadcast_to(block[:, k : k + 1], block.shape)


def row(block, j):
    return jnp.broadcast_to(block[j : j + 1, :], block.shape)


def lower_inverse(gram):
    blocks = R // NB
    sub = lax.broadcasted_iota(jnp.int32, (NB, R), 0)
    col = lax.broadcasted_iota(jnp.int32, (NB, R), 1)
    schur = [gram[NB * i : NB * i + NB, :] for i in range(blocks)]
    aug = [jnp.where(col == sub + NB * i, 1.0, 0.0) for i in range(blocks)]
    out = []
    for kb in range(blocks):
        top, left = schur[kb], aug[kb]
        diag = [lane(top, NB * kb + j) for j in range(NB)]
        below = {i: [lane(schur[i], NB * kb + j) for j in range(NB)] for i in range(kb + 1, blocks)}
        pivots = jnp.ones((NB, R), jnp.float32)
        for j in range(NB):
            pivot = row(diag[j], j)
            inv = 1.0 / pivot
            pivots = jnp.where(sub == j, pivot, pivots)
            mult = jnp.where(sub > j, diag[j] * inv, 0.0)
            ups = [row(diag[jj], j) for jj in range(j + 1, NB)]
            for a, jj in enumerate(range(j + 1, NB)):
                diag[jj] = diag[jj] - mult * ups[a]
            trow, lrow = row(top, j), row(left, j)
            top = top - mult * trow
            left = left - mult * lrow
            for i in range(kb + 1, blocks):
                m = below[i][j] * inv
                for a, jj in enumerate(range(j + 1, NB)):
                    below[i][jj] = below[i][jj] - m * ups[a]
                schur[i] = schur[i] - m * trow
                aug[i] = aug[i] - m * lrow
        out.append(left * lax.rsqrt(pivots))
    return jnp.concatenate(out, axis=0)


def split(x):
    hi = x.astype(jnp.bfloat16)
    rest = x - hi.astype(jnp.float32)
    mid = rest.astype(jnp.bfloat16)
    low = (rest - mid.astype(jnp.float32)).astype(jnp.bfloat16)
    return hi, mid, low


def iterate_kernel(w_ref, start_ref, left_ref, right_ref, wh, wm, wl, yt):
    for r in range(0, B, 128):
        hi, mid, low = split(w_ref[r : r + 128, :])
        wh[r : r + 128, :] = hi
        wm[r : r + 128, :] = mid
        wl[r : r + 128, :] = low

    def mul(a, b, dims):
        return lax.dot_general(a, b, dims, preferred_element_type=jnp.float32)

    def times(block, dims):
        hi, mid, low = split(block)
        three = jnp.concatenate([hi, mid, low], axis=0)
        by_h = mul(three, wh[...], dims)
        by_m = mul(three[: 2 * R], wm[...], dims)
        by_l = mul(hi, wl[...], dims)
        return (by_h[:R] + by_h[R : 2 * R] + by_m[:R]) + (by_h[2 * R :] + by_m[R:] + by_l)

    def half(dims):
        block = yt[...]
        gram = lax.dot_general(block, block, NT, precision=HIGH, preferred_element_type=jnp.float32)
        product = times(block, dims)
        return lower_inverse(gram), block, product

    def apply(inv, block):
        return lax.dot_general(inv, block, NN, precision=HIGH, preferred_element_type=jnp.float32)

    yt[...] = times(start_ref[...].T, NT)

    def sweep(_, carry):
        inv, _, product = half(NN)
        yt[...] = apply(inv, product)
        inv, _, product = half(NT)
        yt[...] = apply(inv, product)
        return carry

    lax.fori_loop(0, ITERS, sweep, 0)
    inv, block, product = half(NN)
    left_ref[...] = (apply(inv, block) * math.sqrt(B)).T
    right_ref[...] = apply(inv, product).T


def iterate(w, start):
    shape = jax.ShapeDtypeStruct((B, R), jnp.float32)
    return pl.pallas_call(
        iterate_kernel,
        out_shape=(shape, shape),
        scratch_shapes=[
            pltpu.VMEM((B, B), jnp.bfloat16),
            pltpu.VMEM((B, B), jnp.bfloat16),
            pltpu.VMEM((B, B), jnp.bfloat16),
            pltpu.VMEM((R, B), jnp.float32),
        ],
        compiler_params=pltpu.CompilerParams(vmem_limit_bytes=56 * 1024 * 1024),
        name="iterate",
    )(w, start)


def shards(tile_left, tile_right, diag_left, diag_right, present, old_left, old_right, start):
    diag_left = lax.all_gather(diag_left[0], "rows", axis=0, tiled=True)
    diag_right = lax.all_gather(diag_right[0], "rows", axis=0, tiled=True)
    weight = present.astype(jnp.float32)[0, 0]
    coupling = jnp.einsum("br,bs->rs", tile_right[0, 0], diag_right, precision=HIGH) * weight
    scaled = -jnp.einsum("br,rs->bs", tile_left[0, 0], coupling, precision=HIGH)
    first = jnp.where(lax.axis_index("past") == 0, 1.0, 0.0)
    lhs = jnp.concatenate([scaled, old_left[0] * first], axis=1)
    rhs = jnp.concatenate([diag_left, old_right[0]], axis=1)
    partial_w = jnp.einsum("bk,ck->bc", lhs, rhs, precision=HIGH)
    w = lax.psum(partial_w, "past")
    left, right = iterate(w, start[0])
    return left[None], right[None]


def solution(mesh):
    placed = (
        P("rows", "past", None, None),
        P("rows", "past", None, None),
        P("past", "rows", None),
        P("past", "rows", None),
        P("rows", "past"),
        P("rows", None, None),
        P("rows", None, None),
        P("rows", None, None),
    )
    return jax.shard_map(
        shards,
        mesh=mesh,
        in_specs=placed,
        out_specs=(P("rows", None, None), P("rows", None, None)),
        check_vma=False,
    )
```

```python
import math

import jax
import jax.numpy as jnp
from jax import lax
from jax.experimental import pallas as pl
from jax.experimental.pallas import tpu as pltpu
from jax.sharding import PartitionSpec as P

B = 1024
R = 128
ITERS = 3
NB = 8
HALF = B // 2
PART = B // 16
SLAB = B // 64
QUART = B // 4

HIGH = lax.Precision.HIGHEST
NN = (((1,), (0,)), ((), ()))
NT = (((1,), (1,)), ((), ()))
TN = (((0,), (0,)), ((), ()))


def lane(block, k):
    return jnp.broadcast_to(block[:, k : k + 1], block.shape)


def row(block, j):
    return jnp.broadcast_to(block[j : j + 1, :], block.shape)


def lower_inverse(gram):
    blocks = R // NB
    sub = lax.broadcasted_iota(jnp.int32, (NB, R), 0)
    col = lax.broadcasted_iota(jnp.int32, (NB, R), 1)
    schur = [gram[NB * i : NB * i + NB, :] for i in range(blocks)]
    aug = [jnp.where(col == sub + NB * i, 1.0, 0.0) for i in range(blocks)]
    out = []
    for kb in range(blocks):
        top, left = schur[kb], aug[kb]
        diag = [lane(top, NB * kb + j) for j in range(NB)]
        below = {i: [lane(schur[i], NB * kb + j) for j in range(NB)] for i in range(kb + 1, blocks)}
        pivots = jnp.ones((NB, R), jnp.float32)
        for j in range(NB):
            pivot = row(diag[j], j)
            inv = 1.0 / pivot
            pivots = jnp.where(sub == j, pivot, pivots)
            mult = jnp.where(sub > j, diag[j] * inv, 0.0)
            ups = [row(diag[jj], j) for jj in range(j + 1, NB)]
            for a, jj in enumerate(range(j + 1, NB)):
                diag[jj] = diag[jj] - mult * ups[a]
            trow, lrow = row(top, j), row(left, j)
            top = top - mult * trow
            left = left - mult * lrow
            for i in range(kb + 1, blocks):
                m = below[i][j] * inv
                for a, jj in enumerate(range(j + 1, NB)):
                    below[i][jj] = below[i][jj] - m * ups[a]
                schur[i] = schur[i] - m * trow
                aug[i] = aug[i] - m * lrow
        out.append(left * lax.rsqrt(pivots))
    return jnp.concatenate(out, axis=0)


def split(x):
    hi = x.astype(jnp.bfloat16)
    rest = x - hi.astype(jnp.float32)
    mid = rest.astype(jnp.bfloat16)
    low = (rest - mid.astype(jnp.float32)).astype(jnp.bfloat16)
    return hi, mid, low


def place():
    p = lax.axis_index("past")
    return p // 16, (p // 2) % 8, p % 2, lax.axis_index("rows")


def shift_rows(value, k):
    return lax.ppermute(value, "rows", [(i, (i + k) % 4) for i in range(4)])


def swap_cores(value):
    return lax.ppermute(value, "past", [(i, i ^ 1) for i in range(64)])


GROUP = [(k, b) for k in (2, 1, 3, 0) for b in (1, 0) if (k, b) != (0, 0)]
FAR = (2, 1, 3)


def send_group(value, k, b):
    pairs = [
        (x * 16 + z * 2 + c, ((x + k) % 4) * 16 + (z ^ b) * 2 + c)
        for x in range(4)
        for z in range(8)
        for c in range(2)
    ]
    return lax.ppermute(value, "past", pairs)


def send_far(value, k):
    pairs = [
        (x * 16 + z * 2 + c, x * 16 + ((z + 2 * k) % 8) * 2 + c)
        for x in range(4)
        for z in range(8)
        for c in range(2)
    ]
    return lax.ppermute(value, "past", pairs)


def f32_dot(a, b, dims):
    return lax.dot_general(a, b, dims, precision=HIGH, preferred_element_type=jnp.float32)


def rows_at(index, size):
    return pl.ds(pl.multiple_of(index * size, size), size)


def couple_kernel(present_ref, right_ref, left_ref, d0, d1, d2, d3, keep_ref, send_ref):
    _, _, c, y = place()
    total = None
    for k, ref in enumerate((d0, d1, d2, d3)):
        part = right_ref[rows_at((y + 4 - k) % 4, QUART), :]
        term = f32_dot(part, ref[...], TN)
        total = term if total is None else total + term
    total = total * -present_ref[0, 0].astype(jnp.float32)
    keep_ref[...] = f32_dot(left_ref[rows_at(c, HALF), :], total, NN)
    send_ref[...] = f32_dot(left_ref[rows_at(1 - c, HALF), :], total, NN)


def couple(present, right, left, pieces):
    shape = jax.ShapeDtypeStruct((HALF, R), jnp.float32)
    vmem = pl.BlockSpec(memory_space=pltpu.VMEM)
    return pl.pallas_call(
        couple_kernel,
        out_shape=(shape, shape),
        in_specs=[pl.BlockSpec(memory_space=pltpu.SMEM)] + [vmem] * 6,
        out_specs=(vmem, vmem),
        name="couple",
    )(present, right, left, *pieces)


def tile_kernel(own_ref, other_ref, down_ref, dother_ref, *outs):
    x, z, _, y = place()
    zb = z % 2
    for j, (k, b) in enumerate([(0, 0)] + GROUP):
        target = ((x + k) % 4) * 2 + (zb + b) % 2
        a = jnp.concatenate([own_ref[rows_at(target, PART), :], other_ref[rows_at(target, PART), :]], axis=1)
        for q in range(4):
            d = jnp.concatenate(
                [down_ref[q * QUART : (q + 1) * QUART, :], dother_ref[q * QUART : (q + 1) * QUART, :]], axis=1
            )
            outs[j][:, rows_at((y + 4 - q) % 4, QUART)] = f32_dot(a, d, NT)


def tile_parts(own, other, down, dother):
    shape = jax.ShapeDtypeStruct((PART, B), jnp.float32)
    return pl.pallas_call(tile_kernel, out_shape=(shape,) * 8, name="tile_parts")(own, other, down, dother)


def near_kernel(*refs):
    ins, outs = refs[:8], refs[8:]
    _, z, _, _ = place()
    for j, k in enumerate((0,) + FAR):
        rows = rows_at((z // 2 + k) % 4, SLAB)
        total = ins[0][rows, :]
        for ref in ins[1:]:
            total = total + ref[rows, :]
        outs[j][...] = total


def near_sum(parts):
    shape = jax.ShapeDtypeStruct((SLAB, B), jnp.float32)
    return pl.pallas_call(near_kernel, out_shape=(shape,) * 4, name="near_sum")(*parts)


def far_kernel(s0, s1, s2, s3, old_left_ref, old_right_ref, out_ref):
    x, z, c, _ = place()
    index = c * 32 + (x * 2 + z % 2) * 4 + z // 2
    old = f32_dot(old_left_ref[rows_at(index, SLAB), :], old_right_ref[...], NT)
    out_ref[...] = old + ((s0[...] + s1[...]) + (s2[...] + s3[...]))


def far_sum(slabs, old_left, old_right):
    shape = jax.ShapeDtypeStruct((SLAB, B), jnp.float32)
    return pl.pallas_call(far_kernel, out_shape=shape, name="far_sum")(*slabs, old_left, old_right)


def iterate_kernel(*refs):
    pieces = refs[:16]
    start_ref, left_ref, right_ref, wh, wm, wl, yt = refs[16:]
    x, z, c, _ = place()
    for h in range(2):
        half_base = (c + h) % 2 * 8
        for j, (k, b) in enumerate([(0, 0)] + GROUP):
            member = ((x + 4 - k) % 4) * 2 + (z % 2 + b) % 2
            for q, far in enumerate((0,) + FAR):
                index = (half_base + member) * 4 + (z // 2 + 4 - far) % 4
                hi, mid, low = split(pieces[h * 8 + j][q * SLAB : (q + 1) * SLAB, :])
                rows = rows_at(index, SLAB)
                wh[rows, :] = hi
                wm[rows, :] = mid
                wl[rows, :] = low

    def mul(a, b, dims):
        return lax.dot_general(a, b, dims, preferred_element_type=jnp.float32)

    def times(block, dims):
        hi, mid, low = split(block)
        three = jnp.concatenate([hi, mid, low], axis=0)
        by_h = mul(three, wh[...], dims)
        by_m = mul(three[: 2 * R], wm[...], dims)
        by_l = mul(hi, wl[...], dims)
        return (by_h[:R] + by_h[R : 2 * R] + by_m[:R]) + (by_h[2 * R :] + by_m[R:] + by_l)

    def half(dims):
        block = yt[...]
        gram = lax.dot_general(block, block, NT, precision=HIGH, preferred_element_type=jnp.float32)
        product = times(block, dims)
        return lower_inverse(gram), block, product

    def apply(inv, block):
        return lax.dot_general(inv, block, NN, precision=HIGH, preferred_element_type=jnp.float32)

    yt[...] = times(start_ref[...].T, NT)

    def sweep(_, carry):
        inv, _, product = half(NN)
        yt[...] = apply(inv, product)
        inv, _, product = half(NT)
        yt[...] = apply(inv, product)
        return carry

    lax.fori_loop(0, ITERS, sweep, 0)
    inv, block, product = half(NN)
    left_ref[...] = (apply(inv, block) * math.sqrt(B)).T
    right_ref[...] = apply(inv, product).T


def iterate(pieces, start):
    shape = jax.ShapeDtypeStruct((B, R), jnp.float32)
    return pl.pallas_call(
        iterate_kernel,
        out_shape=(shape, shape),
        scratch_shapes=[
            pltpu.VMEM((B, B), jnp.bfloat16),
            pltpu.VMEM((B, B), jnp.bfloat16),
            pltpu.VMEM((B, B), jnp.bfloat16),
            pltpu.VMEM((R, B), jnp.float32),
        ],
        compiler_params=pltpu.CompilerParams(vmem_limit_bytes=56 * 1024 * 1024),
        name="iterate",
    )(*pieces, start)


def shards(tile_left, tile_right, diag_left, diag_right, present, old_left, old_right, start):
    rights = [diag_right[0]] + [shift_rows(diag_right[0], k) for k in (1, 2, 3)]
    lefts = [diag_left[0]] + [shift_rows(diag_left[0], k) for k in (1, 2, 3)]
    own, away = couple(present, tile_right[0, 0], tile_left[0, 0], rights)
    other = swap_cores(away)
    down = jnp.concatenate(lefts, axis=0)
    dother = swap_cores(down)
    parts = tile_parts(own, other, down, dother)
    got = [parts[0]] + [send_group(v, k, b) for v, (k, b) in zip(parts[1:], GROUP)]
    slabs = near_sum(got)
    got = [slabs[0]] + [send_far(v, k) for v, k in zip(slabs[1:], FAR)]
    slab = far_sum(got, old_left[0], old_right[0])
    piece = jnp.concatenate([slab] + [send_far(slab, k) for k in FAR], axis=0)
    mine = [piece] + [send_group(piece, k, b) for k, b in GROUP]
    theirs = [swap_cores(v) for v in mine]
    left, right = iterate(mine + theirs, start[0])
    return left[None], right[None]


def solution(mesh):
    placed = (
        P("rows", "past", None, None),
        P("rows", "past", None, None),
        P("past", "rows", None),
        P("past", "rows", None),
        P("rows", "past"),
        P("rows", None, None),
        P("rows", None, None),
        P("rows", None, None),
    )
    return jax.shard_map(
        shards,
        mesh=mesh,
        in_specs=placed,
        out_specs=(P("rows", None, None), P("rows", None, None)),
        check_vma=False,
    )
```

```python
import functools
import math

import jax
import jax.numpy as jnp
from jax import lax
from jax.experimental import pallas as pl
from jax.experimental.pallas import tpu as pltpu
from jax.sharding import PartitionSpec as P

B = 1024
R = 128
ITERS = 3
NB = 8
HALF = B // 2
PART = B // 16
SLAB = B // 64
QUART = B // 4

HIGH = lax.Precision.HIGHEST
NN = (((1,), (0,)), ((), ()))
NT = (((1,), (1,)), ((), ()))
TN = (((0,), (0,)), ((), ()))


def lane(block, k):
    return jnp.broadcast_to(block[:, k : k + 1], block.shape)


def row(block, j):
    return jnp.broadcast_to(block[j : j + 1, :], block.shape)


NEAR = 3


def exact_parts(x):
    hi, mid, low = split(x)
    return hi.astype(jnp.float32), mid.astype(jnp.float32), low.astype(jnp.float32)


def lower_inverse(gram):
    blocks = R // NB
    sub = lax.broadcasted_iota(jnp.int32, (NB, R), 0)
    col = lax.broadcasted_iota(jnp.int32, (NB, R), 1)
    work = [gram[NB * i : NB * i + NB, :] for i in range(blocks)]

    def columns(block, k):
        return [lane(block, NB * k + j) for j in range(NB)]

    out = []
    next_diag, next_below = columns(work[0], 0), columns(work[1], 0)
    for kb in range(blocks):
        here = (col >= NB * kb) & (col < NB * kb + NB)
        near = range(kb + 1, min(blocks, kb + 1 + NEAR))
        diag = next_diag
        below = {i: next_below if i == kb + 1 else columns(work[i], kb) for i in near}
        if kb + 1 < blocks:
            next_diag = columns(work[kb + 1], kb + 1)
        if kb + 2 < blocks:
            next_below = columns(work[kb + 2], kb + 1)
        top = jnp.where(here, jnp.where(col == sub + NB * kb, 1.0, 0.0), work[kb])
        for i in range(kb + 1, blocks):
            work[i] = jnp.where(here, 0.0, work[i])
        pivots = inverses = None
        diag_sums, below_sums = [0.0] * NB, [0.0] * NB
        for j in range(NB):
            pivot = row(diag[j], j)
            inv = 1.0 / pivot
            pivots = pivot if j == 0 else jnp.where(sub >= j, pivot, pivots)
            inverses = inv if j == 0 else jnp.where(sub >= j, inv, inverses)
            ups = [row(diag[jj], j) for jj in range(j + 1, NB)]
            trow = row(top, j)
            if j < NB - 1:
                mult = jnp.where(sub > j, diag[j] * inv, 0.0)
                for jj, up in enumerate(ups, j + 1):
                    diag[jj] = diag[jj] - mult * up
                top = top - mult * trow
            mults = {}
            for i in near:
                mults[i] = below[i][j] * inv
                for jj, up in enumerate(ups, j + 1):
                    below[i][jj] = below[i][jj] - mults[i] * up
                work[i] = work[i] - mults[i] * trow
            if kb + 1 < blocks:
                for q in range(NB):
                    up = row(below[kb + 1][j], q)
                    diag_sums[q] = diag_sums[q] + mults[kb + 1] * up
                    if kb + 2 < blocks:
                        below_sums[q] = below_sums[q] + mults[kb + 2] * up
        if kb + 1 < blocks:
            next_diag = [a - s for a, s in zip(next_diag, diag_sums)]
        if kb + 2 < blocks:
            next_below = [a - s for a, s in zip(next_below, below_sums)]
        out.append(jnp.where(col < NB * kb + NB, top * lax.rsqrt(pivots), 0.0))
        far = kb + 1 + NEAR
        if far < blocks:
            lh, lm, ll = exact_parts(top * inverses)
            th, tm, tl = exact_parts(top)
            lhs = jnp.concatenate([lh, lh, lm, lh, ll, lm], axis=0).astype(jnp.bfloat16)
            rhs = jnp.concatenate([th, tm, th, tl, th, tm], axis=0).astype(jnp.bfloat16)
            update = lax.dot_general(lhs, rhs, TN, preferred_element_type=jnp.float32)
            for i in range(far, blocks):
                work[i] = work[i] - update[NB * i : NB * i + NB, :]
    return jnp.concatenate(out, axis=0)


def split(x):
    hi = x.astype(jnp.bfloat16)
    rest = x - hi.astype(jnp.float32)
    mid = rest.astype(jnp.bfloat16)
    low = (rest - mid.astype(jnp.float32)).astype(jnp.bfloat16)
    return hi, mid, low


def place():
    p = lax.axis_index("past")
    return p // 16, (p // 2) % 8, p % 2, lax.axis_index("rows")


def shift_rows(value, k):
    return lax.ppermute(value, "rows", [(i, (i + k) % 4) for i in range(4)])


def swap_cores(value):
    return lax.ppermute(value, "past", [(i, i ^ 1) for i in range(64)])


GROUP = [(0, 1), (1, 0), (3, 0), (1, 1), (3, 1), (2, 0), (2, 1)]
FAR = (2, 1, 3)


def send_group(value, k, b):
    pairs = [
        (x * 16 + z * 2 + c, ((x + k) % 4) * 16 + (z ^ b) * 2 + c)
        for x in range(4)
        for z in range(8)
        for c in range(2)
    ]
    return lax.ppermute(value, "past", pairs)


def send_far(value, k):
    pairs = [
        (x * 16 + z * 2 + c, x * 16 + ((z + 2 * k) % 8) * 2 + c)
        for x in range(4)
        for z in range(8)
        for c in range(2)
    ]
    return lax.ppermute(value, "past", pairs)


def f32_dot(a, b, dims):
    return lax.dot_general(a, b, dims, precision=HIGH, preferred_element_type=jnp.float32)


def rows_at(index, size):
    return pl.ds(pl.multiple_of(index * size, size), size)


def couple_kernel(present_ref, right_ref, left_ref, d0, d1, d2, d3, keep_ref, send_ref):
    _, _, c, y = place()
    total = None
    for k, ref in zip((0,) + FAR, (d0, d1, d2, d3)):
        part = right_ref[rows_at((y + 4 - k) % 4, QUART), :]
        term = f32_dot(part, ref[...], TN)
        total = term if total is None else total + term
    total = total * -present_ref[0, 0].astype(jnp.float32)
    keep_ref[...] = f32_dot(left_ref[rows_at(c, HALF), :], total, NN)
    send_ref[...] = f32_dot(left_ref[rows_at(1 - c, HALF), :], total, NN)


def couple(present, right, left, pieces):
    shape = jax.ShapeDtypeStruct((HALF, R), jnp.float32)
    vmem = pl.BlockSpec(memory_space=pltpu.VMEM)
    return pl.pallas_call(
        couple_kernel,
        out_shape=(shape, shape),
        in_specs=[pl.BlockSpec(memory_space=pltpu.SMEM)] + [vmem] * 6,
        out_specs=(vmem, vmem),
        name="couple",
    )(present, right, left, *pieces)


MEMBERS = [(0, 0)] + GROUP


def tile_kernel(first, *refs):
    own_ref, other_ref = refs[:2]
    downs, dother_ref, outs, d_ref = refs[2:6], refs[6], refs[7:11], refs[11]
    x, z, _, y = place()
    for q, k in enumerate((0,) + FAR):
        rows = rows_at((y + 4 - k) % 4, QUART)
        d_ref[rows, :R] = downs[q][...]
        d_ref[rows, R:] = dother_ref[q * QUART : (q + 1) * QUART, :]
    blocks = []
    for k, b in (MEMBERS[4:], MEMBERS[:4])[1 - first]:
        rows = rows_at(((x + k) % 4) * 2 + (z % 2 + b) % 2, PART)
        blocks.append(jnp.concatenate([own_ref[rows, :], other_ref[rows, :]], axis=1))
    out = f32_dot(jnp.concatenate(blocks, axis=0), d_ref[...], NT)
    for j in range(4):
        outs[j][...] = out[j * PART : (j + 1) * PART, :]


def tile_parts(own, other, downs, dother, first):
    shape = jax.ShapeDtypeStruct((PART, B), jnp.float32)
    return pl.pallas_call(
        functools.partial(tile_kernel, first),
        out_shape=(shape,) * 4,
        scratch_shapes=[pltpu.VMEM((B, 2 * R), jnp.float32)],
        name="tile_parts",
    )(own, other, *downs, dother)


def old_kernel(old_left_ref, old_right_ref, out_ref):
    x, z, c, _ = place()
    index = c * 32 + (x * 2 + z % 2) * 4 + z // 2
    out_ref[...] = f32_dot(old_left_ref[rows_at(index, SLAB), :], old_right_ref[...], NT)


def old_slab(old_left, old_right):
    shape = jax.ShapeDtypeStruct((SLAB, B), jnp.float32)
    return pl.pallas_call(old_kernel, out_shape=shape, name="old_slab")(old_left, old_right)


def near_kernel(*refs):
    ins, outs = refs[:8], refs[8:]
    _, z, _, _ = place()
    for j, k in enumerate((0,) + FAR):
        rows = rows_at((z // 2 + k) % 4, SLAB)
        total = ins[0][rows, :]
        for ref in ins[1:]:
            total = total + ref[rows, :]
        outs[j][...] = total


def near_sum(parts):
    shape = jax.ShapeDtypeStruct((SLAB, B), jnp.float32)
    return pl.pallas_call(near_kernel, out_shape=(shape,) * 4, name="near_sum")(*parts)


def far_kernel(s0, s1, s2, s3, old_ref, out_ref):
    out_ref[...] = old_ref[...] + ((s0[...] + s1[...]) + (s2[...] + s3[...]))


def far_sum(slabs, old):
    shape = jax.ShapeDtypeStruct((SLAB, B), jnp.float32)
    return pl.pallas_call(far_kernel, out_shape=shape, name="far_sum")(*slabs, old)


def iterate_kernel(*refs):
    mine, theirs = refs[:8], refs[8:10]
    start_ref, left_ref, right_ref, wh, wm, wl, yt = refs[10:]
    x, z, c, _ = place()
    for h in range(2):
        half_base = (c + h) % 2 * 8
        for j, (k, b) in enumerate([(0, 0)] + GROUP):
            member = ((x + 4 - k) % 4) * 2 + (z % 2 + b) % 2
            for q, far in enumerate((0,) + FAR):
                index = (half_base + member) * 4 + (z // 2 + 4 - far) % 4
                ref, at = (theirs[j // 4], j % 4 * PART) if h else (mine[j], 0)
                hi, mid, low = split(ref[at + q * SLAB : at + (q + 1) * SLAB, :])
                rows = rows_at(index, SLAB)
                wh[rows, :] = hi
                wm[rows, :] = mid
                wl[rows, :] = low

    def mul(a, b, dims):
        return lax.dot_general(a, b, dims, preferred_element_type=jnp.float32)

    def times(block, dims):
        hi, mid, low = split(block)
        three = jnp.concatenate([hi, mid, low], axis=0)
        by_h = mul(three, wh[...], dims)
        by_m = mul(three[: 2 * R], wm[...], dims)
        by_l = mul(hi, wl[...], dims)
        return (by_h[:R] + by_h[R : 2 * R] + by_m[:R]) + (by_h[2 * R :] + by_m[R:] + by_l)

    def half(dims):
        block = yt[...]
        gram = lax.dot_general(block, block, NT, precision=HIGH, preferred_element_type=jnp.float32)
        product = times(block, dims)
        return lower_inverse(gram), block, product

    def apply(inv, block):
        return lax.dot_general(inv, block, NN, precision=HIGH, preferred_element_type=jnp.float32)

    yt[...] = times(start_ref[...].T, NT)

    def sweep(step, carry):
        inv, block, product = half(NN)

        @pl.when(step == ITERS)
        def _():
            left_ref[...] = (apply(inv, block) * math.sqrt(B)).T
            right_ref[...] = apply(inv, product).T

        @pl.when(step < ITERS)
        def _():
            yt[...] = apply(inv, product)
            inv2, _, product2 = half(NT)
            yt[...] = apply(inv2, product2)

        return carry

    lax.fori_loop(0, ITERS + 1, sweep, 0)


def iterate(pieces, start):
    shape = jax.ShapeDtypeStruct((B, R), jnp.float32)
    return pl.pallas_call(
        iterate_kernel,
        out_shape=(shape, shape),
        scratch_shapes=[
            pltpu.VMEM((B, B), jnp.bfloat16),
            pltpu.VMEM((B, B), jnp.bfloat16),
            pltpu.VMEM((B, B), jnp.bfloat16),
            pltpu.VMEM((R, B), jnp.float32),
        ],
        compiler_params=pltpu.CompilerParams(vmem_limit_bytes=56 * 1024 * 1024),
        name="iterate",
    )(*pieces, start)


def shards(tile_left, tile_right, diag_left, diag_right, present, old_left, old_right, start):
    rights = [diag_right[0]] + [shift_rows(diag_right[0], k) for k in (2, 1, 3)]
    mine, rights[1] = lax.optimization_barrier((diag_left[0], rights[1]))
    lefts = [mine] + [shift_rows(mine, k) for k in (2, 1, 3)]
    own, away = couple(present, tile_right[0, 0], tile_left[0, 0], rights)
    other = swap_cores(away)
    dother = swap_cores(jnp.concatenate(lefts, axis=0))
    far_parts = tile_parts(own, other, lefts, dother, 1)
    old = old_slab(old_left[0], old_right[0])
    sent = [send_group(v, k, b) for v, (k, b) in zip(far_parts, MEMBERS[4:])]
    parts = tile_parts(own, other, lefts, dother, 0)
    sent += [send_group(v, k, b) for v, (k, b) in zip(parts[1:], MEMBERS[1:])]
    got = [parts[0]] + sent
    slabs = near_sum(got)
    got = [slabs[0]] + [send_far(v, k) for v, k in zip(slabs[1:], FAR)]
    slab = far_sum(got, old)
    piece = jnp.concatenate([slab] + [send_far(slab, k) for k in FAR], axis=0)
    mine = [piece] + [send_group(piece, k, b) for k, b in GROUP]
    theirs = [swap_cores(jnp.concatenate(part, axis=0)) for part in (mine[:4], mine[4:])]
    left, right = iterate(mine + theirs, start[0])
    return left[None], right[None]


def solution(mesh):
    placed = (
        P("rows", "past", None, None),
        P("rows", "past", None, None),
        P("past", "rows", None),
        P("past", "rows", None),
        P("rows", "past"),
        P("rows", None, None),
        P("rows", None, None),
        P("rows", None, None),
    )
    return jax.shard_map(
        shards,
        mesh=mesh,
        in_specs=placed,
        out_specs=(P("rows", None, None), P("rows", None, None)),
        check_vma=False,
    )
```

```python
import functools
import math

import jax
import jax.numpy as jnp
from jax import lax
from jax.experimental import pallas as pl
from jax.experimental.pallas import tpu as pltpu
from jax.sharding import PartitionSpec as P

B = 1024
R = 128
ITERS = 3
NB = 8
HALF = B // 2
PART = B // 16
SLAB = B // 64
QUART = B // 4

HIGH = lax.Precision.HIGHEST
NN = (((1,), (0,)), ((), ()))
NT = (((1,), (1,)), ((), ()))
TN = (((0,), (0,)), ((), ()))


def lane(block, k):
    return jnp.broadcast_to(block[:, k : k + 1], block.shape)


def row(block, j):
    return jnp.broadcast_to(block[j : j + 1, :], block.shape)


NEAR = 3


def exact_parts(x):
    hi, mid, low = split(x)
    return hi.astype(jnp.float32), mid.astype(jnp.float32), low.astype(jnp.float32)


def lower_inverse(gram):
    blocks = R // NB
    sub = lax.broadcasted_iota(jnp.int32, (NB, R), 0)
    col = lax.broadcasted_iota(jnp.int32, (NB, R), 1)
    work = [gram[NB * i : NB * i + NB, :] for i in range(blocks)]

    def columns(block, k):
        return [lane(block, NB * k + j) for j in range(NB)]

    out = []
    next_diag, next_below = columns(work[0], 0), columns(work[1], 0)
    for kb in range(blocks):
        here = (col >= NB * kb) & (col < NB * kb + NB)
        near = range(kb + 1, min(blocks, kb + 1 + NEAR))
        diag = next_diag
        below = {i: next_below if i == kb + 1 else columns(work[i], kb) for i in near}
        if kb + 1 < blocks:
            next_diag = columns(work[kb + 1], kb + 1)
        if kb + 2 < blocks:
            next_below = columns(work[kb + 2], kb + 1)
        top = jnp.where(here, jnp.where(col == sub + NB * kb, 1.0, 0.0), work[kb])
        for i in range(kb + 1, blocks):
            work[i] = jnp.where(here, 0.0, work[i])
        pivots = inverses = None
        diag_sums, below_sums = [0.0] * NB, [0.0] * NB
        for j in range(NB):
            pivot = row(diag[j], j)
            inv = 1.0 / pivot
            pivots = pivot if j == 0 else jnp.where(sub >= j, pivot, pivots)
            inverses = inv if j == 0 else jnp.where(sub >= j, inv, inverses)
            ups = [row(diag[jj], j) for jj in range(j + 1, NB)]
            trow = row(top, j)
            if j < NB - 1:
                mult = jnp.where(sub > j, diag[j] * inv, 0.0)
                for jj, up in enumerate(ups, j + 1):
                    diag[jj] = diag[jj] - mult * up
                top = top - mult * trow
            mults = {}
            for i in near:
                mults[i] = below[i][j] * inv
                for jj, up in enumerate(ups, j + 1):
                    below[i][jj] = below[i][jj] - mults[i] * up
                work[i] = work[i] - mults[i] * trow
            if kb + 1 < blocks:
                for q in range(NB):
                    up = row(below[kb + 1][j], q)
                    diag_sums[q] = diag_sums[q] + mults[kb + 1] * up
                    if kb + 2 < blocks:
                        below_sums[q] = below_sums[q] + mults[kb + 2] * up
        if kb + 1 < blocks:
            next_diag = [a - s for a, s in zip(next_diag, diag_sums)]
        if kb + 2 < blocks:
            next_below = [a - s for a, s in zip(next_below, below_sums)]
        out.append(jnp.where(col < NB * kb + NB, top * lax.rsqrt(pivots), 0.0))
        far = kb + 1 + NEAR
        if far < blocks:
            lh, lm, ll = exact_parts(top * inverses)
            th, tm, tl = exact_parts(top)
            lhs = jnp.concatenate([lh, lh, lm, lh, ll, lm], axis=0).astype(jnp.bfloat16)
            rhs = jnp.concatenate([th, tm, th, tl, th, tm], axis=0).astype(jnp.bfloat16)
            update = lax.dot_general(lhs, rhs, TN, preferred_element_type=jnp.float32)
            for i in range(far, blocks):
                work[i] = work[i] - update[NB * i : NB * i + NB, :]
    return jnp.concatenate(out, axis=0)


def split(x):
    hi = x.astype(jnp.bfloat16)
    rest = x - hi.astype(jnp.float32)
    mid = rest.astype(jnp.bfloat16)
    low = (rest - mid.astype(jnp.float32)).astype(jnp.bfloat16)
    return hi, mid, low


def place():
    p = lax.axis_index("past")
    return p // 16, (p // 2) % 8, p % 2, lax.axis_index("rows")


def shift_rows(value, k):
    return lax.ppermute(value, "rows", [(i, (i + k) % 4) for i in range(4)])


def swap_cores(value):
    return lax.ppermute(value, "past", [(i, i ^ 1) for i in range(64)])


GROUP = [(0, 1), (1, 0), (3, 0), (1, 1), (3, 1), (2, 0), (2, 1)]
FAR = (2, 1, 3)


def send_group(value, k, b):
    pairs = [
        (x * 16 + z * 2 + c, ((x + k) % 4) * 16 + (z ^ b) * 2 + c)
        for x in range(4)
        for z in range(8)
        for c in range(2)
    ]
    return lax.ppermute(value, "past", pairs)


def send_far(value, k):
    pairs = [
        (x * 16 + z * 2 + c, x * 16 + ((z + 2 * k) % 8) * 2 + c)
        for x in range(4)
        for z in range(8)
        for c in range(2)
    ]
    return lax.ppermute(value, "past", pairs)


def f32_dot(a, b, dims):
    return lax.dot_general(a, b, dims, precision=HIGH, preferred_element_type=jnp.float32)


def rows_at(index, size):
    return pl.ds(pl.multiple_of(index * size, size), size)


def couple_kernel(present_ref, right_ref, left_ref, d0, d1, d2, d3, keep_ref, send_ref):
    _, _, c, y = place()
    total = None
    for k, ref in zip((0,) + FAR, (d0, d1, d2, d3)):
        part = right_ref[rows_at((y + 4 - k) % 4, QUART), :]
        term = f32_dot(part, ref[QUART:, :], TN)
        total = term if total is None else total + term
    total = total * -present_ref[0, 0].astype(jnp.float32)
    keep_ref[...] = f32_dot(left_ref[rows_at(c, HALF), :], total, NN)
    send_ref[...] = f32_dot(left_ref[rows_at(1 - c, HALF), :], total, NN)


def couple(present, right, left, pieces):
    shape = jax.ShapeDtypeStruct((HALF, R), jnp.float32)
    vmem = pl.BlockSpec(memory_space=pltpu.VMEM)
    return pl.pallas_call(
        couple_kernel,
        out_shape=(shape, shape),
        in_specs=[pl.BlockSpec(memory_space=pltpu.SMEM)] + [vmem] * 6,
        out_specs=(vmem, vmem),
        name="couple",
    )(present, right, left, *pieces)


MEMBERS = [(0, 0)] + GROUP


def tile_kernel(first, *refs):
    own_ref, other_ref = refs[:2]
    downs, dother_ref, outs, d_ref = refs[2:6], refs[6], refs[7:11], refs[11]
    x, z, _, y = place()
    for q, k in enumerate((0,) + FAR):
        rows = rows_at((y + 4 - k) % 4, QUART)
        d_ref[rows, :R] = downs[q][:QUART, :]
        d_ref[rows, R:] = dother_ref[q * QUART : (q + 1) * QUART, :]
    blocks = []
    for k, b in (MEMBERS[4:], MEMBERS[:4])[1 - first]:
        rows = rows_at(((x + k) % 4) * 2 + (z % 2 + b) % 2, PART)
        blocks.append(jnp.concatenate([own_ref[rows, :], other_ref[rows, :]], axis=1))
    out = f32_dot(jnp.concatenate(blocks, axis=0), d_ref[...], NT)
    for j in range(4):
        outs[j][...] = out[j * PART : (j + 1) * PART, :]


def tile_parts(own, other, downs, dother, first):
    shape = jax.ShapeDtypeStruct((PART, B), jnp.float32)
    return pl.pallas_call(
        functools.partial(tile_kernel, first),
        out_shape=(shape,) * 4,
        scratch_shapes=[pltpu.VMEM((B, 2 * R), jnp.float32)],
        name="tile_parts",
    )(own, other, *downs, dother)


def old_kernel(old_left_ref, old_right_ref, out_ref):
    x, z, c, _ = place()
    index = c * 32 + (x * 2 + z % 2) * 4 + z // 2
    out_ref[...] = f32_dot(old_left_ref[rows_at(index, SLAB), :], old_right_ref[...], NT)


def old_slab(old_left, old_right):
    shape = jax.ShapeDtypeStruct((SLAB, B), jnp.float32)
    return pl.pallas_call(old_kernel, out_shape=shape, name="old_slab")(old_left, old_right)


def near_kernel(*refs):
    ins, outs = refs[:8], refs[8:]
    _, z, _, _ = place()
    for j, k in enumerate((0,) + FAR):
        rows = rows_at((z // 2 + k) % 4, SLAB)
        total = ins[0][rows, :]
        for ref in ins[1:]:
            total = total + ref[rows, :]
        outs[j][...] = total


def near_sum(parts):
    shape = jax.ShapeDtypeStruct((SLAB, B), jnp.float32)
    return pl.pallas_call(near_kernel, out_shape=(shape,) * 4, name="near_sum")(*parts)


def far_kernel(s0, s1, s2, s3, old_ref, out_ref):
    out_ref[...] = old_ref[...] + ((s0[...] + s1[...]) + (s2[...] + s3[...]))


def far_sum(slabs, old):
    shape = jax.ShapeDtypeStruct((SLAB, B), jnp.float32)
    return pl.pallas_call(far_kernel, out_shape=shape, name="far_sum")(*slabs, old)


def iterate_kernel(*refs):
    mine, theirs = refs[:8], refs[8:10]
    start_ref, left_ref, right_ref, wh, wm, wl, yt = refs[10:]
    x, z, c, _ = place()
    for h in range(2):
        half_base = (c + h) % 2 * 8
        for j, (k, b) in enumerate([(0, 0)] + GROUP):
            member = ((x + 4 - k) % 4) * 2 + (z % 2 + b) % 2
            for q, far in enumerate((0,) + FAR):
                index = (half_base + member) * 4 + (z // 2 + 4 - far) % 4
                ref, at = (theirs[j // 4], j % 4 * PART) if h else (mine[j], 0)
                hi, mid, low = split(ref[at + q * SLAB : at + (q + 1) * SLAB, :])
                rows = rows_at(index, SLAB)
                wh[rows, :] = hi
                wm[rows, :] = mid
                wl[rows, :] = low

    def mul(a, b, dims):
        return lax.dot_general(a, b, dims, preferred_element_type=jnp.float32)

    def times(block, dims):
        hi, mid, low = split(block)
        three = jnp.concatenate([hi, mid, low], axis=0)
        by_h = mul(three, wh[...], dims)
        by_m = mul(three[: 2 * R], wm[...], dims)
        by_l = mul(hi, wl[...], dims)
        return (by_h[:R] + by_h[R : 2 * R] + by_m[:R]) + (by_h[2 * R :] + by_m[R:] + by_l)

    def half(dims):
        block = yt[...]
        gram = lax.dot_general(block, block, NT, precision=HIGH, preferred_element_type=jnp.float32)
        product = times(block, dims)
        return lower_inverse(gram), block, product

    def apply(inv, block):
        return lax.dot_general(inv, block, NN, precision=HIGH, preferred_element_type=jnp.float32)

    yt[...] = times(start_ref[...].T, NT)

    def sweep(step, carry):
        inv, block, product = half(NN)

        @pl.when(step == ITERS)
        def _():
            left_ref[...] = (apply(inv, block) * math.sqrt(B)).T
            right_ref[...] = apply(inv, product).T

        @pl.when(step < ITERS)
        def _():
            yt[...] = apply(inv, product)
            inv2, _, product2 = half(NT)
            yt[...] = apply(inv2, product2)

        return carry

    lax.fori_loop(0, ITERS + 1, sweep, 0)


def iterate(pieces, start):
    shape = jax.ShapeDtypeStruct((B, R), jnp.float32)
    return pl.pallas_call(
        iterate_kernel,
        out_shape=(shape, shape),
        scratch_shapes=[
            pltpu.VMEM((B, B), jnp.bfloat16),
            pltpu.VMEM((B, B), jnp.bfloat16),
            pltpu.VMEM((B, B), jnp.bfloat16),
            pltpu.VMEM((R, B), jnp.float32),
        ],
        compiler_params=pltpu.CompilerParams(vmem_limit_bytes=56 * 1024 * 1024),
        name="iterate",
    )(*pieces, start)


def shards(tile_left, tile_right, diag_left, diag_right, present, old_left, old_right, start):
    mine = jnp.concatenate([diag_left[0], diag_right[0]], axis=0)
    factors = [mine] + [shift_rows(mine, k) for k in FAR]
    dother = swap_cores(jnp.concatenate([f[:QUART] for f in factors], axis=0))
    own, away = couple(present, tile_right[0, 0], tile_left[0, 0], factors)
    other = swap_cores(away)
    far_parts = tile_parts(own, other, factors, dother, 1)
    old = old_slab(old_left[0], old_right[0])
    sent = [send_group(v, k, b) for v, (k, b) in zip(far_parts, MEMBERS[4:])]
    parts = tile_parts(own, other, factors, dother, 0)
    sent += [send_group(v, k, b) for v, (k, b) in zip(parts[1:], MEMBERS[1:])]
    got = [parts[0]] + sent
    slabs = near_sum(got)
    got = [slabs[0]] + [send_far(v, k) for v, k in zip(slabs[1:], FAR)]
    slab = far_sum(got, old)
    piece = jnp.concatenate([slab] + [send_far(slab, k) for k in FAR], axis=0)
    mine = [piece] + [send_group(piece, k, b) for k, b in GROUP]
    theirs = [swap_cores(jnp.concatenate(part, axis=0)) for part in (mine[:4], mine[4:])]
    left, right = iterate(mine + theirs, start[0])
    return left[None], right[None]


def solution(mesh):
    placed = (
        P("rows", "past", None, None),
        P("rows", "past", None, None),
        P("past", "rows", None),
        P("past", "rows", None),
        P("rows", "past"),
        P("rows", None, None),
        P("rows", None, None),
        P("rows", None, None),
    )
    return jax.shard_map(
        shards,
        mesh=mesh,
        in_specs=placed,
        out_specs=(P("rows", None, None), P("rows", None, None)),
        check_vma=False,
    )
```
